32 devices in a mesh: rep: 8 (over z, y), grp: 4 (over x, core).
Axes of the slice: x: 2, y: 2, z: 4, core: 2. Of those that a mesh axis runs over, the one named last changes fastest.
Arguments:
- tokens: bfloat16 [3648, 1152], P(('rep', 'grp')), may hold values from -6 to 6
- cotangent: bfloat16 [3648, 1152], P(('rep', 'grp')), may hold values from -6 to 6
- slice_sizes: int32 [32], replicated, may hold values from 113 to 114, as said below
- gain_one: float32 [1152], replicated, may hold values from 0.1 to 1.9
- shift_one: float32 [1152], replicated, may hold values from -3 to 3
- attn_in: bfloat16 [3456, 1152], P('grp')
- attn_bias: float32 [2, 1152], replicated, may hold values from -3 to 3
- attn_out: bfloat16 [1152, 1152], P('grp'), may hold values from -1 to 1
- out_bias: float32 [1152], replicated, may hold values from -3 to 3
- gain_two: float32 [1152], replicated, may hold values from 0.1 to 1.9
- shift_two: float32 [1152], replicated, may hold values from -3 to 3
- mlp_up: bfloat16 [4304, 1152], P('grp'), may hold values from -0.1875 to 0.1875
- up_bias: float32 [4304], replicated, may hold values from -3 to 3
- mlp_down: bfloat16 [4304, 1152], P('grp'), may hold values from -0.09375 to 0.09375
- down_bias: float32 [1152], replicated, may hold values from -3 to 3
Outputs:
- block_output: bfloat16 [3648, 1152], P(('rep', 'grp'))
- input_grad: float32 [3648, 1152], P(('rep', 'grp'))
- dgain_one: float32 [1152], replicated
- dshift_one: float32 [1152], replicated
- dattn_in: float32 [3456, 1152], P('grp', 'rep')
- dattn_bias: float32 [2, 1152], replicated
- dattn_out: float32 [1152, 1152], P('grp', 'rep')
- dout_bias: float32 [1152], replicated
- dgain_two: float32 [1152], replicated
- dshift_two: float32 [1152], replicated
- dmlp_up: float32 [4304, 1152], P('grp', 'rep')
- dup_bias: float32 [4304], replicated
- dmlp_down: float32 [4304, 1152], P('grp', 'rep')
- ddown_bias: float32 [1152], replicated
The draws below stay inside these ranges and needn't reach their ends.
Inputs may be any that keep to these rules, and one draw needn't show every extreme that they name: slice_sizes sums to 3645; every entry is 113 or one more.
All inputs are finite; a program needn't handle non-finite values.
Results may differ from the reference program's by a relative error of at most 0.012.
Values may be sent and summed in bfloat16 or wider, within the bound.
A program may use at most 192 MiB of HBM per device.

```python
import jax
import jax.numpy as jnp
from jax import lax

D = 1152
H = 16
HD = 72
FF = 4304
IMG = 729
SHARDS = 32
NIMG = 5
TOKENS = 3645
SLOTS = 3648


def draw_slice_sizes(key, part):
    ranking = jax.random.permutation(key, SHARDS)
    extra = (ranking < TOKENS % SHARDS).astype(jnp.int32)
    return (TOKENS // SHARDS + extra).astype(jnp.int32)


def draw_attn_in(key, part):
    base = jax.random.normal(key, (3 * D, D), jnp.float32) * D ** (-0.5)
    return base.astype(jnp.bfloat16)


def raised(values, own_key, source, target, shards_of, factor):
    owner, partner = [(jnp.arange(values.shape[axis_at]) // (values.shape[axis_at] // shards_of)).reshape([-1 if axis == axis_at else 1 for axis in range(values.ndim)]) for axis_at in (source, target)]
    chosen = jax.random.permutation(own_key, shards_of)[partner]
    strong = (owner == chosen) | (owner == (partner + shards_of // 2) % shards_of)
    return jnp.where(strong, factor * values, values)


def steps_of(stream_key, dims, pieces, smallest, largest):
    def one(axis_at, blocks):
        heights = jax.random.uniform(jax.random.fold_in(jax.random.fold_in(stream_key, 6), axis_at), (blocks,), jnp.float32, smallest / len(pieces), largest / len(pieces))
        return jnp.repeat(jnp.exp(heights), dims[axis_at] // blocks).reshape((-1,) + (1,) * (len(dims) - axis_at - 1))

    gain = one(*pieces[0])
    for cut in pieces[1:]:
        gain = gain * one(*cut)
    return gain


def normal_values(own_key, extent, scale, reach, cuts=(), held_as=jnp.bfloat16):
    gain = steps_of(own_key, extent, cuts, -0.22, 0.18) if cuts else 1.0
    values = jax.random.normal(own_key, extent, jnp.float32) * scale * gain
    return jnp.minimum(jnp.maximum(values, -reach), reach).astype(held_as)


def noise_with(rng, extent, width, bound, split, heavy, kind=jnp.bfloat16):
    result = width * jax.random.normal(rng, extent, jnp.float32)
    if split:
        result = result * steps_of(rng, extent, split, -0.22, 0.18)
    return jnp.clip(raised(result, jax.random.fold_in(rng, 3), *heavy), -bound, bound).astype(kind)


def setup_inputs(seed: int = 0) -> dict:
    splits = jax.random.split(jax.random.key(seed), 16)
    tokens = noise_with(splits[0], (SLOTS, D), 1.0, 6.0, ((0, 32),), (0, 1, 32, 2.75))
    cotangent = noise_with(splits[1], (SLOTS, D), 1.0, 6.0, ((0, 32),), (0, 1, 32, 2.75))
    slice_sizes = draw_slice_sizes(jax.random.fold_in(splits[15], 71), 0)
    gain_one = jnp.clip(1.0 + 0.18 * jax.random.normal(splits[3], (D,), jnp.float32), 0.1, 1.9)
    shift_one = normal_values(splits[4], (D,), 0.5, 3.0, (), jnp.float32)
    attn_in = draw_attn_in(jax.random.fold_in(splits[15], 71), 0)
    attn_bias = normal_values(splits[6], (2, D), 0.5, 3.0, (), jnp.float32)
    attn_out = normal_values(splits[7], (D, D), (D // 27) ** -0.5, 1.0, ((0, 4),))
    out_bias = normal_values(splits[8], (D,), 0.5, 3.0, (), jnp.float32)
    gain_two = jnp.clip(1.0 + 0.18 * jax.random.normal(splits[9], (D,), jnp.float32), 0.1, 1.9)
    shift_two = normal_values(splits[10], (D,), 0.5, 3.0, (), jnp.float32)
    mlp_up = normal_values(splits[11], (FF, D), D ** -0.5, 0.1875, ((0, 4),))
    up_bias = normal_values(splits[12], (FF,), 0.5, 3.0, (), jnp.float32)
    mlp_down = normal_values(splits[13], (FF, D), FF ** -0.5, 0.09375, ((0, 4),))
    down_bias = normal_values(splits[14], (D,), 0.5, 3.0, (), jnp.float32)
    return {"tokens": tokens, "cotangent": cotangent, "slice_sizes": slice_sizes, "gain_one": gain_one, "shift_one": shift_one, "attn_in": attn_in, "attn_bias": attn_bias, "attn_out": attn_out, "out_bias": out_bias, "gain_two": gain_two, "shift_two": shift_two, "mlp_up": mlp_up, "up_bias": up_bias, "mlp_down": mlp_down, "down_bias": down_bias}


EPSILON = 1e-06
SQRT_TWO_PI = 0.7978845608028654
CUBIC = 0.044715

def norm_forward(rows, gain_row, shift_row):
    centered = rows - lax.optimization_barrier(jnp.mean(rows, axis=-1, keepdims=True))
    inverse = lax.rsqrt(lax.optimization_barrier(jnp.mean(centered * centered, axis=-1, keepdims=True)) + EPSILON)
    normed = centered * inverse
    return (normed, inverse, normed * gain_row + shift_row)

def norm_backward(dscaled, normed, inverse, gain_row):
    dnormed = dscaled * gain_row
    return inverse * (dnormed - lax.optimization_barrier(jnp.mean(dnormed, axis=-1, keepdims=True)) - normed * lax.optimization_barrier(jnp.mean(dnormed * normed, axis=-1, keepdims=True)))

def gelu_parts(before):
    inside = SQRT_TWO_PI * (before + CUBIC * before * before * before)
    tangent = jnp.tanh(inside)
    activated = 0.5 * before * (1.0 + tangent)
    derivative = 0.5 * (1.0 + tangent) + 0.5 * before * (1.0 - tangent * tangent) * SQRT_TWO_PI * (1.0 + 3.0 * CUBIC * before * before)
    return (activated, derivative)

def reference(tokens, cotangent, slice_sizes, gain_one, shift_one, attn_in, attn_bias, attn_out, out_bias, gain_two, shift_two, mlp_up, up_bias, mlp_down, down_bias):
    shards = slice_sizes.shape[0]
    capacity = tokens.shape[0] // shards
    starts = (jnp.cumsum(slice_sizes) - slice_sizes).astype(jnp.int32)
    slot_shard = jnp.repeat(jnp.arange(shards, dtype=jnp.int32), capacity)
    slot_row = jnp.tile(jnp.arange(capacity, dtype=jnp.int32), shards)
    slot_live = slot_row < slice_sizes[slot_shard]
    slot_token = jnp.where(slot_live, starts[slot_shard] + slot_row, TOKENS).astype(jnp.int32)
    stream = jnp.zeros((TOKENS, D), tokens.dtype).at[slot_token].set(tokens, mode='drop')
    cot_stream = jnp.zeros((TOKENS, D), cotangent.dtype).at[slot_token].set(cotangent, mode='drop')
    score_scale = HD ** (-0.5)
    bias_full = jnp.concatenate([attn_bias[0], jnp.zeros((D,), jnp.float32), attn_bias[1]])

    def image_pass(carry, inputs):
        rows, cot_rows = inputs
        tokens_f = rows.astype(jnp.float32)
        normed_one, inverse_one, scaled_one = norm_forward(tokens_f, gain_one, shift_one)
        first = scaled_one.astype(jnp.bfloat16)
        projected = jnp.dot(first, attn_in.T, preferred_element_type=jnp.float32) + bias_full
        queries = projected[:, :D].astype(jnp.bfloat16).reshape(IMG, H, HD)
        keys3 = projected[:, D:2 * D].astype(jnp.bfloat16).reshape(IMG, H, HD)
        values3 = projected[:, 2 * D:].astype(jnp.bfloat16).reshape(IMG, H, HD)
        scores = jnp.einsum('qhd,khd->hqk', queries.astype(jnp.float32), keys3.astype(jnp.float32)) * score_scale
        highest = lax.optimization_barrier(jnp.max(scores, axis=-1, keepdims=True))
        logsum = highest + jnp.log(lax.optimization_barrier(jnp.sum(jnp.exp(scores - highest), axis=-1, keepdims=True)))
        probs = jnp.exp(scores - logsum)
        weights = probs.astype(jnp.bfloat16)
        mixed = jnp.einsum('hqk,khd->qhd', weights.astype(jnp.float32), values3.astype(jnp.float32)).astype(jnp.bfloat16).reshape(IMG, D)
        resid = tokens_f + jnp.dot(mixed, attn_out, preferred_element_type=jnp.float32) + out_bias
        normed_two, inverse_two, scaled_two = norm_forward(resid, gain_two, shift_two)
        second = scaled_two.astype(jnp.bfloat16)
        before = jnp.dot(second, mlp_up.T, preferred_element_type=jnp.float32) + up_bias
        activated, derivative = gelu_parts(before)
        hidden = activated.astype(jnp.bfloat16)
        final = resid + jnp.dot(hidden, mlp_down, preferred_element_type=jnp.float32) + down_bias
        dfinal = cot_rows.astype(jnp.float32)
        dmlp_down = jnp.dot(hidden.T, cot_rows, preferred_element_type=jnp.float32)
        dbefore = jnp.dot(cot_rows, mlp_down.T, preferred_element_type=jnp.float32) * derivative
        dbefore_b = dbefore.astype(jnp.bfloat16)
        dmlp_up = jnp.dot(dbefore_b.T, second, preferred_element_type=jnp.float32)
        dsecond = jnp.dot(dbefore_b, mlp_up, preferred_element_type=jnp.float32)
        dresid = dfinal + norm_backward(dsecond, normed_two, inverse_two, gain_two)
        dresid_b = dresid.astype(jnp.bfloat16)
        dattn_out = jnp.dot(mixed.T, dresid_b, preferred_element_type=jnp.float32)
        dmixed = jnp.dot(dresid_b, attn_out.T, preferred_element_type=jnp.float32).astype(jnp.bfloat16)
        dmixed3 = dmixed.reshape(IMG, H, HD)
        delta = lax.optimization_barrier(jnp.sum(dmixed3.astype(jnp.float32) * mixed.reshape(IMG, H, HD).astype(jnp.float32), axis=-1)).T
        dprob = jnp.einsum('qhd,khd->hqk', dmixed3.astype(jnp.float32), values3.astype(jnp.float32))
        dscore = (probs * (dprob - delta[:, :, None]) * score_scale).astype(jnp.bfloat16)
        dquery = jnp.einsum('hqk,khd->qhd', dscore.astype(jnp.float32), keys3.astype(jnp.float32)).reshape(IMG, D)
        dkey = jnp.einsum('hqk,qhd->khd', dscore.astype(jnp.float32), queries.astype(jnp.float32)).reshape(IMG, D)
        dvalue = jnp.einsum('hqk,qhd->khd', weights.astype(jnp.float32), dmixed3.astype(jnp.float32)).reshape(IMG, D)
        dprojected = jnp.concatenate([dquery, dkey, dvalue], axis=1).astype(jnp.bfloat16)
        dattn_in = jnp.dot(dprojected.T, first, preferred_element_type=jnp.float32)
        dfirst = jnp.dot(dprojected, attn_in, preferred_element_type=jnp.float32)
        input_rows = dresid + norm_backward(dfirst, normed_one, inverse_one, gain_one)
        terms = (lax.optimization_barrier(jnp.sum(dfirst * normed_one, axis=0)), lax.optimization_barrier(jnp.sum(dfirst, axis=0)), dattn_in, jnp.stack([lax.optimization_barrier(jnp.sum(dquery, axis=0)), lax.optimization_barrier(jnp.sum(dvalue, axis=0))]), dattn_out, lax.optimization_barrier(jnp.sum(dresid, axis=0)), lax.optimization_barrier(jnp.sum(dsecond * normed_two, axis=0)), lax.optimization_barrier(jnp.sum(dsecond, axis=0)), dmlp_up, lax.optimization_barrier(jnp.sum(dbefore, axis=0)), dmlp_down, lax.optimization_barrier(jnp.sum(dfinal, axis=0)))
        carry = tuple((total + term for total, term in zip(carry, terms)))
        return (carry, (final.astype(jnp.bfloat16), input_rows))
    zero_f = jnp.float32(0.0)
    init = (jnp.zeros((D,), jnp.float32), jnp.zeros((D,), jnp.float32), jnp.zeros((3 * D, D), jnp.float32), jnp.zeros((2, D), jnp.float32), jnp.zeros((D, D), jnp.float32), jnp.zeros((D,), jnp.float32), jnp.zeros((D,), jnp.float32), jnp.zeros((D,), jnp.float32), jnp.zeros((FF, D), jnp.float32), jnp.zeros((FF,), jnp.float32), jnp.zeros((FF, D), jnp.float32), jnp.zeros((D,), jnp.float32) + zero_f)
    totals, (out_images, grad_images) = lax.scan(image_pass, init, (stream.reshape(NIMG, IMG, D), cot_stream.reshape(NIMG, IMG, D)))
    out_stream = out_images.reshape(TOKENS, D)
    grad_stream = grad_images.reshape(TOKENS, D)
    fetch = jnp.minimum(slot_token, TOKENS - 1).astype(jnp.int32)
    live_col = slot_live[:, None]
    block_output = jnp.where(live_col, out_stream[fetch], jnp.zeros_like(out_stream[fetch]))
    input_grad = jnp.where(live_col, grad_stream[fetch], jnp.zeros_like(grad_stream[fetch]))
    dgain_one, dshift_one, dattn_in, dattn_bias, dattn_out, dout_bias, dgain_two, dshift_two, dmlp_up, dup_bias, dmlp_down, ddown_bias = totals
    return (block_output, input_grad, dgain_one, dshift_one, dattn_in, dattn_bias, dattn_out, dout_bias, dgain_two, dshift_two, dmlp_up, dup_bias, dmlp_down, ddown_bias)
```

```python
import functools

import jax
import jax.numpy as jnp
from jax import lax
from jax.experimental import pallas as pl
from jax.sharding import PartitionSpec as P

H = 16
HD = 72
IMG = 729


EPSILON = 1e-06
SQRT_TWO_PI = 0.7978845608028654
CUBIC = 0.044715
NEGATIVE = -1e30


def norm_forward(rows, gain_row, shift_row):
    centered = rows - jnp.mean(rows, axis=-1, keepdims=True)
    inverse = lax.rsqrt(jnp.mean(centered * centered, axis=-1, keepdims=True) + EPSILON)
    normed = centered * inverse
    return (normed, inverse, normed * gain_row + shift_row)


def norm_backward(dscaled, normed, inverse, gain_row):
    dnormed = dscaled * gain_row
    return inverse * (
        dnormed
        - jnp.mean(dnormed, axis=-1, keepdims=True)
        - normed * jnp.mean(dnormed * normed, axis=-1, keepdims=True)
    )


def gelu_parts(before):
    inside = SQRT_TWO_PI * (before + CUBIC * before * before * before)
    tangent = jnp.tanh(inside)
    activated = 0.5 * before * (1.0 + tangent)
    derivative = 0.5 * (1.0 + tangent) + 0.5 * before * (1.0 - tangent * tangent) * SQRT_TWO_PI * (
        1.0 + 3.0 * CUBIC * before * before
    )
    return (activated, derivative)


def dot_over(left, right, left_axis, right_axis):
    return lax.dot_general(
        left, right, (((left_axis,), (right_axis,)), ((), ())), preferred_element_type=jnp.float32
    )


def forward_kernel(q_ref, k_ref, v_ref, qi_ref, ki_ref, mixed_ref, lse_ref):
    allowed = qi_ref[0] == ki_ref[0]
    raw = dot_over(q_ref[0], k_ref[0], 1, 1) * (HD ** (-0.5))
    scores = jnp.where(allowed, raw, NEGATIVE)
    highest = jnp.max(scores, axis=-1, keepdims=True)
    powers = jnp.where(allowed, jnp.exp(scores - highest), 0.0)
    total = jnp.sum(powers, axis=-1, keepdims=True)
    total = jnp.where(total > 0.0, total, 1.0)
    weights = (powers * (1.0 / total)).astype(jnp.bfloat16)
    mixed_ref[0] = dot_over(weights, v_ref[0], 1, 0).astype(jnp.bfloat16)
    lse_ref[0] = highest + jnp.log(total)


def backward_kernel(
    q_ref, k_ref, v_ref, qi_ref, ki_ref, mixed_ref, lse_ref, dmixed_ref, dq_ref, dk_ref, dv_ref
):
    allowed = qi_ref[0] == ki_ref[0]
    raw = dot_over(q_ref[0], k_ref[0], 1, 1) * (HD ** (-0.5))
    probs = jnp.where(allowed, jnp.exp(jnp.where(allowed, raw - lse_ref[0], 0.0)), 0.0)
    dmixed = dmixed_ref[0]
    delta = jnp.sum(
        dmixed.astype(jnp.float32) * mixed_ref[0].astype(jnp.float32), axis=-1, keepdims=True
    )
    dprob = dot_over(dmixed, v_ref[0], 1, 1)
    dscore = (probs * (dprob - delta) * (HD ** (-0.5))).astype(jnp.bfloat16)
    dq_ref[0] = dot_over(dscore, k_ref[0], 1, 0)
    dk_ref[0] = dot_over(dscore, q_ref[0], 0, 0)
    dv_ref[0] = dot_over(probs.astype(jnp.bfloat16), dmixed, 0, 0)


def blocked(shape):
    return pl.BlockSpec((1,) + shape[1:], lambda b: (b, 0, 0))


def block_call(kernel, args, outs):
    return pl.pallas_call(
        kernel,
        grid=(args[0].shape[0],),
        in_specs=[blocked(a.shape) for a in args],
        out_specs=[blocked(o.shape) for o in outs],
        out_shape=outs,
    )(*args)


def per_device(
    tokens,
    cotangent,
    slice_sizes,
    gain_one,
    shift_one,
    attn_in,
    attn_bias,
    attn_out,
    out_bias,
    gain_two,
    shift_two,
    mlp_up,
    up_bias,
    mlp_down,
    down_bias,
):
    capacity, width = tokens.shape
    reps, groups = lax.axis_size("rep"), lax.axis_size("grp")
    devices = reps * groups
    turns = H // groups
    segments = reps // turns
    reach = (IMG - 2 + capacity - 1) // (capacity - 1)
    rows = groups * capacity
    halo = reach * capacity
    segment_rows = H * capacity
    window = rows + 2 * halo
    rep, member = lax.axis_index("rep"), lax.axis_index("grp")
    device = rep * groups + member
    segment, turn = rep // turns, rep % turns
    head = member * turns + turn
    kinds = attn_in.shape[0] // HD
    rep_sets = [[s * turns + i for i in range(turns)] for s in range(segments)]
    all_sets = [[s * H + i for i in range(H)] for s in range(segments)]
    spread = functools.partial(
        lax.all_to_all, split_axis=0, concat_axis=0, tiled=True
    )

    def gathered(block):
        return lax.all_gather(block, "grp", axis=0, tiled=True)

    def scattered(partial_rows):
        blocks = partial_rows.astype(jnp.bfloat16).reshape(groups, capacity, width)
        return jnp.sum(spread(blocks, "grp").astype(jnp.float32), axis=0)

    def rep_summed(grad_rows):
        return lax.psum_scatter(
            grad_rows.astype(jnp.bfloat16), "rep", scatter_dimension=1, tiled=True
        ).astype(jnp.float32)

    starts = jnp.cumsum(slice_sizes) - slice_sizes
    own_count = slice_sizes[device]
    row_index = jnp.arange(capacity, dtype=jnp.int32)
    live_col = (row_index < own_count)[:, None]

    images = jnp.where(
        row_index[None, :] < slice_sizes[:, None],
        (starts[:, None] + row_index[None, :]) // IMG,
        -2,
    )
    padding = jnp.full((reach, capacity), -2, jnp.int32)
    images = jnp.concatenate([padding, images, padding], axis=0)
    images = lax.dynamic_slice_in_dim(images, segment * H, H + 2 * reach, 0).reshape(-1)
    query_image = images[halo : halo + segment_rows]
    query_image = jnp.where(query_image < 0, -1, query_image).reshape(turns, rows, 1)

    def windows(whole):
        return jnp.stack([whole[b * rows : b * rows + window] for b in range(turns)])

    key_image = windows(images).reshape(turns, 1, window)

    dfinal_b = jnp.where(live_col, cotangent, jnp.zeros_like(cotangent))
    dfinal = dfinal_b.astype(jnp.float32)
    tokens_f = tokens.astype(jnp.float32)
    group_normed, _, group_scaled = norm_forward(
        gathered(tokens).astype(jnp.float32), gain_one, shift_one
    )
    first = group_scaled.astype(jnp.bfloat16)
    normed_one, inverse_one, _ = norm_forward(tokens_f, gain_one, shift_one)
    dfinal_all = gathered(dfinal_b)
    bias_full = jnp.concatenate([attn_bias[0], jnp.zeros((width,), jnp.float32), attn_bias[1]])
    own_bias = lax.dynamic_slice_in_dim(bias_full, member * kinds * HD, kinds * HD, 0)
    projected = (dot_over(first, attn_in, 1, 1) + own_bias).astype(jnp.bfloat16)
    padded = jnp.pad(projected, ((0, 0), (0, (H - kinds) * HD)))
    shift = (member * kinds) % H
    rolled = lax.dynamic_slice_in_dim(
        jnp.concatenate([padded, padded], axis=1), ((H - shift) % H) * HD, H * HD, 1
    )
    outgoing = rolled.reshape(rows, groups, turns, HD).transpose(2, 1, 0, 3)
    incoming = spread(
        outgoing.reshape(H, rows, HD), ("rep", "grp"), axis_index_groups=all_sets
    ).reshape(turns, groups, rows, HD)

    def kind_of(kind):
        return lax.dynamic_index_in_dim(incoming, (kind * H + head) // kinds, 1, keepdims=False)

    queries = kind_of(0)
    keyvalue = jnp.concatenate([kind_of(1), kind_of(2)], axis=-1).reshape(segment_rows, 2 * HD)
    onward = [(r, r + turns) for r in range(reps - turns)]
    backward = [(r + turns, r) for r in range(reps - turns)]
    before_rows = lax.ppermute(keyvalue[segment_rows - halo :], "rep", onward)
    after_rows = lax.ppermute(keyvalue[:halo], "rep", backward)
    neighbours = jnp.concatenate([before_rows, keyvalue, after_rows], axis=0)
    keys = windows(neighbours[:, :HD])
    values = windows(neighbours[:, HD:])
    shared = (queries, keys, values, query_image, key_image)
    mixed, lse = block_call(
        forward_kernel,
        shared,
        [
            jax.ShapeDtypeStruct((turns, rows, HD), jnp.bfloat16),
            jax.ShapeDtypeStruct((turns, rows, 1), jnp.float32),
        ],
    )
    mixed_own = (
        spread(mixed, "rep", axis_index_groups=rep_sets)
        .transpose(1, 0, 2)
        .reshape(rows, turns * HD)
    )
    resid = tokens_f + scattered(dot_over(mixed_own, attn_out, 1, 0)) + out_bias
    normed_two, inverse_two, scaled_two = norm_forward(resid, gain_two, shift_two)
    second = gathered(scaled_two.astype(jnp.bfloat16))
    hidden_rows = mlp_up.shape[0]
    own_up_bias = lax.dynamic_slice_in_dim(up_bias, member * hidden_rows, hidden_rows, 0)
    before = dot_over(second, mlp_up, 1, 1) + own_up_bias
    activated, derivative = gelu_parts(before)
    hidden = activated.astype(jnp.bfloat16)
    dbefore = dot_over(dfinal_all, mlp_down, 1, 1) * derivative
    dbefore_b = dbefore.astype(jnp.bfloat16)
    dsecond = scattered(dot_over(dbefore_b, mlp_up, 1, 0))
    dresid = dfinal + norm_backward(dsecond, normed_two, inverse_two, gain_two)
    dresid_all = gathered(dresid.astype(jnp.bfloat16))
    dmixed_own = dot_over(dresid_all, attn_out, 1, 1).astype(jnp.bfloat16)
    dmixed = spread(
        dmixed_own.reshape(rows, turns, HD).transpose(1, 0, 2), "rep", axis_index_groups=rep_sets
    )
    final = resid + scattered(dot_over(hidden, mlp_down, 1, 0)) + down_bias
    block_output = jnp.where(live_col, final, 0.0).astype(jnp.bfloat16)
    summed = rep_summed(
        jnp.concatenate(
            [
                dot_over(dbefore_b, second, 0, 0).astype(jnp.bfloat16),
                dot_over(hidden, dfinal_all, 0, 0).astype(jnp.bfloat16),
                dot_over(mixed_own, dresid_all, 0, 0).astype(jnp.bfloat16),
            ],
            axis=0,
        )
    )
    dmlp_up = summed[:hidden_rows]
    dmlp_down = summed[hidden_rows : 2 * hidden_rows]
    dattn_out = summed[2 * hidden_rows :]

    dq, dk, dv = block_call(
        backward_kernel,
        shared + (mixed, lse, dmixed),
        [
            jax.ShapeDtypeStruct((turns, rows, HD), jnp.float32),
            jax.ShapeDtypeStruct((turns, window, HD), jnp.float32),
            jax.ShapeDtypeStruct((turns, window, HD), jnp.float32),
        ],
    )
    dkv = jnp.concatenate([dk, dv], axis=-1)
    span = segment_rows + 2 * halo
    dneighbours = sum(
        jnp.pad(dkv[b], ((b * rows, span - window - b * rows), (0, 0))) for b in range(turns)
    )
    to_before = lax.ppermute(dneighbours[:halo].astype(jnp.bfloat16), "rep", backward)
    to_after = lax.ppermute(dneighbours[halo + segment_rows :].astype(jnp.bfloat16), "rep", onward)
    dkeyvalue = (
        dneighbours[halo : halo + segment_rows]
        + jnp.pad(to_before.astype(jnp.float32), ((segment_rows - halo, 0), (0, 0)))
        + jnp.pad(to_after.astype(jnp.float32), ((0, segment_rows - halo), (0, 0)))
    ).astype(jnp.bfloat16)
    dqkv = jnp.stack(
        [
            dq.astype(jnp.bfloat16),
            dkeyvalue[:, :HD].reshape(turns, rows, HD),
            dkeyvalue[:, HD:].reshape(turns, rows, HD),
            jnp.zeros((turns, rows, HD), jnp.bfloat16),
        ]
    )
    pieces = []
    for g in range(groups):
        kind = (g * kinds - head + H - 1) // H
        fits = (kind * H + head < (g + 1) * kinds) & (kind < 3)
        pieces.append(
            lax.dynamic_index_in_dim(dqkv, jnp.where(fits, kind, 3), 0, keepdims=False)
        )
    outgoing = jnp.stack(pieces, axis=1).reshape(H, rows, HD)
    incoming = spread(outgoing, ("rep", "grp"), axis_index_groups=all_sets)
    by_head = (
        incoming.reshape(turns, groups, rows, HD).transpose(2, 1, 0, 3).reshape(rows, H * HD)
    )
    dprojected = lax.dynamic_slice_in_dim(
        jnp.concatenate([by_head, by_head], axis=1), shift * HD, kinds * HD, 1
    )
    dattn_in = rep_summed(dot_over(dprojected, first, 0, 0))
    dfirst_partial = dot_over(dprojected, attn_in, 1, 0)
    dfirst = scattered(dfirst_partial)
    input_grad = jnp.where(
        live_col, dresid + norm_backward(dfirst, normed_one, inverse_one, gain_one), 0.0
    )
    dbias = jnp.stack([jnp.sum(dq, axis=(0, 1)), jnp.sum(dv, axis=(0, 1))])
    dattn_bias = lax.dynamic_update_slice_in_dim(
        jnp.zeros((2, width), jnp.float32), dbias, head * HD, 1
    )
    dup_bias = lax.dynamic_update_slice_in_dim(
        jnp.zeros(up_bias.shape, jnp.float32), jnp.sum(dbefore, axis=0), member * hidden_rows, 0
    )
    dgain_one, dshift_one, dattn_bias, dout_bias, dgain_two, dshift_two, dup_bias, ddown_bias = (
        lax.psum(
            (
                jnp.sum(dfirst_partial * group_normed, axis=0),
                jnp.sum(dfirst_partial, axis=0),
                dattn_bias,
                jnp.sum(dresid, axis=0),
                jnp.sum(dsecond * normed_two, axis=0),
                jnp.sum(dsecond, axis=0),
                dup_bias,
                jnp.sum(dfinal, axis=0),
            ),
            ("rep", "grp"),
        )
    )
    return (
        block_output,
        input_grad,
        dgain_one,
        dshift_one,
        dattn_in,
        dattn_bias,
        dattn_out,
        dout_bias,
        dgain_two,
        dshift_two,
        dmlp_up,
        dup_bias,
        dmlp_down,
        ddown_bias,
    )


def solution(mesh):
    in_specs = (
        P(("rep", "grp"), None),
        P(("rep", "grp"), None),
        P(),
        P(),
        P(),
        P("grp", None),
        P(),
        P("grp", None),
        P(),
        P(),
        P(),
        P("grp", None),
        P(),
        P("grp", None),
        P(),
    )
    out_specs = (
        P(("rep", "grp"), None),
        P(("rep", "grp"), None),
        P(),
        P(),
        P("grp", "rep"),
        P(),
        P("grp", "rep"),
        P(),
        P(),
        P(),
        P("grp", "rep"),
        P(),
        P("grp", "rep"),
        P(),
    )
    return jax.shard_map(
        per_device, mesh=mesh, in_specs=in_specs, out_specs=out_specs, check_vma=False
    )
```
